32 devices in a mesh: dp: 4 (over y, x), ctx: 2 (over core), head: 4 (over z).
Axes of the slice: x: 2, y: 2, z: 4, core: 2. Of those that a mesh axis runs over, the one named last changes fastest.
Arguments:
- inputs: float32 [4, 2048, 768], P('dp', ('ctx', 'head')), may hold values from -6 to 6
- cotangent: float32 [4, 2048, 768], P('dp', ('ctx', 'head')), may hold values from -6 to 6
- head_offsets: int32 [4, 12], replicated, may hold values from 0 to 5, as said below
- w_qkv: bfloat16 [768, 2304], P(('dp', 'ctx', 'head')), may hold values from -0.3125 to 0.3125
- b_query: bfloat16 [768], P(('dp', 'ctx', 'head')), may hold values from -1.75 to 1.75
- b_value: bfloat16 [768], P(('dp', 'ctx', 'head')), may hold values from -0.625 to 0.625
- w_out: bfloat16 [768, 768], P(('dp', 'ctx', 'head')), may hold values from -0.21875 to 0.21875
- b_out: bfloat16 [768], P(('dp', 'ctx', 'head')), may hold values from -1.75 to 1.75
- w_in: bfloat16 [768, 3072], P(('dp', 'ctx', 'head')), may hold values from -0.21875 to 0.21875
- b_in: bfloat16 [3072], P(('dp', 'ctx', 'head')), may hold values from -1.75 to 1.75
- w_down: bfloat16 [3072, 768], P(('dp', 'ctx', 'head')), may hold values from -0.109375 to 0.109375
- b_down: bfloat16 [768], P(('dp', 'ctx', 'head')), may hold values from -1.75 to 1.75
- gain_pre: bfloat16 [768], P(('dp', 'ctx', 'head')), may hold values from 0.25 to 1.75
- gain_attn: bfloat16 [768], P(('dp', 'ctx', 'head')), may hold values from 0.25 to 1.75
- gain_ffn_pre: bfloat16 [768], P(('dp', 'ctx', 'head')), may hold values from 0.25 to 1.75
- gain_ffn_mid: bfloat16 [3072], P(('dp', 'ctx', 'head')), may hold values from 0.25 to 1.75
Outputs:
- outputs: float32 [4, 2048, 768], P('dp', ('ctx', 'head'))
- grad_inputs: float32 [4, 2048, 768], P('dp', ('ctx', 'head'))
- grad_w_qkv: float32 [768, 2304], P(('dp', 'ctx', 'head'))
- grad_b_query: float32 [768], P(('dp', 'ctx', 'head'))
- grad_b_value: float32 [768], P(('dp', 'ctx', 'head'))
- grad_w_out: float32 [768, 768], P(('dp', 'ctx', 'head'))
- grad_b_out: float32 [768], P(('dp', 'ctx', 'head'))
- grad_w_in: float32 [768, 3072], P(('dp', 'ctx', 'head'))
- grad_b_in: float32 [3072], P(('dp', 'ctx', 'head'))
- grad_w_down: float32 [3072, 768], P(('dp', 'ctx', 'head'))
- grad_b_down: float32 [768], P(('dp', 'ctx', 'head'))
- grad_gain_pre: float32 [768], P(('dp', 'ctx', 'head'))
- grad_gain_attn: float32 [768], P(('dp', 'ctx', 'head'))
- grad_gain_ffn_pre: float32 [768], P(('dp', 'ctx', 'head'))
- grad_gain_ffn_mid: float32 [3072], P(('dp', 'ctx', 'head'))
The draws below stay inside these ranges and needn't reach their ends.
Inputs may be any that keep to these rules, and one draw needn't show every extreme that they name: `head_offsets`: row 0 is 0; row b (b = 1, 2, 3) holds offsets below the b-th of 2, 4, 6.
All inputs are finite; a program needn't handle non-finite values.
Results may differ from the reference program's by a relative error of at most 0.02.
Values may be sent and summed in bfloat16 or wider, within the bound.
A program may use at most 128 MiB of HBM per device.

```python
import math
import jax
import jax.numpy as jnp
from jax import lax

D = 768
HEADS = 12
HEAD_DIM = 64
FF = 3072
SEGMENT = 2048
BLOCK = 256
DILATION_SECOND = 2
DILATION_THIRD = 4
DILATION_FOURTH = 6
SEQS = 4
LEN = 2048


def draw_head_offsets(key, part):
    segment_dilation_rates = (1, DILATION_SECOND, DILATION_THIRD, DILATION_FOURTH)
    rows_out = []
    for branch in range(4):
        shuffled = jax.random.permutation(jax.random.fold_in(key, 17 + branch), HEADS)
        rows_out.append(shuffled % segment_dilation_rates[branch])
    return jnp.stack(rows_out).astype(jnp.int32)


def with_spikes(values, own_key, source, target, shards_of, factor):
    def block_of(position):
        return (jnp.arange(values.shape[position]) // (values.shape[position] // shards_of)).reshape((-1,) + (1,) * (values.ndim - 1 - position))

    one_side = jax.random.permutation(own_key, shards_of)[block_of(target)]
    other_side = (block_of(target) + shards_of // 2) % shards_of
    return jnp.where((block_of(source) == one_side) | (block_of(source) == other_side), factor * values, values)


def block_scale(own_key, shape, shards, low, top_value):
    loudness, own = 1.0, jax.random.fold_in(own_key, 6)
    for position, parts in shards:
        steps = jnp.exp(jax.random.uniform(jax.random.fold_in(own, position), (parts,), jnp.float32, low / len(shards), top_value / len(shards)))
        loudness = loudness * jnp.repeat(steps, shape[position] // parts).reshape([-1 if axis == position else 1 for axis in range(len(shape))])
    return loudness


def normal_values(own_key, shape, scale, most, cuts=(), kind=jnp.bfloat16):
    values = scale * jax.random.normal(own_key, shape, jnp.float32)
    if cuts:
        values = values * block_scale(own_key, shape, cuts, -0.22, 0.18)
    return jnp.clip(values, -most, most).astype(kind)


def bell_draw_with(own_key, extent, scale, bound, split, heavy, kind=jnp.bfloat16):
    drawn = scale * jax.random.normal(own_key, extent, jnp.float32)
    if split:
        drawn = drawn * block_scale(own_key, extent, split, -0.22, 0.18)
    return jnp.clip(with_spikes(drawn, jax.random.fold_in(own_key, 3), *heavy), -bound, bound).astype(kind)


def setup_inputs(seed: int = 0) -> dict:
    streams_of = jax.random.split(jax.random.key(seed), 17)
    inputs = normal_values(streams_of[0], (SEQS, LEN, D), 1.0, 6.0, ((0, 4), (1, 8)), jnp.float32)
    cotangent = bell_draw_with(streams_of[1], (SEQS, LEN, D), 1.0, 6.0, ((0, 4), (1, 8)), (1, 2, 8, 2.0), jnp.float32)
    head_offsets = draw_head_offsets(jax.random.fold_in(streams_of[16], 71), 0)
    w_qkv = normal_values(streams_of[3], (D, 3 * D), (D // 2) ** -0.5, 0.3125, ((0, 32),))
    b_query = normal_values(streams_of[4], (D,), 0.3, 1.75, ((0, 32),))
    b_value = normal_values(streams_of[5], (D,), 0.1, 0.625, ((0, 32),))
    w_out = normal_values(streams_of[6], (D, D), D ** -0.5, 0.21875, ((0, 32),))
    b_out = normal_values(streams_of[7], (D,), 0.3, 1.75, ((0, 32),))
    w_in = normal_values(streams_of[8], (D, FF), D ** -0.5, 0.21875, ((0, 32),))
    b_in = normal_values(streams_of[9], (FF,), 0.3, 1.75, ((0, 32),))
    w_down = normal_values(streams_of[10], (FF, D), FF ** -0.5, 0.109375, ((0, 32),))
    b_down = normal_values(streams_of[11], (D,), 0.3, 1.75, ((0, 32),))
    gain_pre = jnp.clip(1.0 + 0.15 * jax.random.normal(streams_of[12], (D,), jnp.float32), 0.25, 1.75).astype(jnp.bfloat16)
    gain_attn = jnp.clip(1.0 + 0.15 * jax.random.normal(streams_of[13], (D,), jnp.float32), 0.25, 1.75).astype(jnp.bfloat16)
    gain_ffn_pre = jnp.clip(1.0 + 0.15 * jax.random.normal(streams_of[14], (D,), jnp.float32), 0.25, 1.75).astype(jnp.bfloat16)
    gain_ffn_mid = jnp.clip(1.0 + 0.15 * jax.random.normal(streams_of[15], (FF,), jnp.float32), 0.25, 1.75).astype(jnp.bfloat16)
    return {"inputs": inputs, "cotangent": cotangent, "head_offsets": head_offsets, "w_qkv": w_qkv, "b_query": b_query, "b_value": b_value, "w_out": w_out, "b_out": b_out, "w_in": w_in, "b_in": b_in, "w_down": w_down, "b_down": b_down, "gain_pre": gain_pre, "gain_attn": gain_attn, "gain_ffn_pre": gain_ffn_pre, "gain_ffn_mid": gain_ffn_mid}


epsilon = 1e-05

@jax.custom_vjp
def low(v):
    return lax.optimization_barrier(v.astype(jnp.bfloat16)).astype(jnp.float32)

@jax.custom_vjp
def low_back(v):
    return v

def low_keep(v):
    return (low(v), None)

def low_pass(kept, grad):
    return (grad,)

def back_keep(v):
    return (v, None)

def back_low(kept, grad):
    return (low(grad),)
low.defvjp(low_keep, low_pass)
low_back.defvjp(back_keep, back_low)

def layer_norm(values, gain_vec):
    centre = values - lax.optimization_barrier(jnp.mean(values, axis=-1, keepdims=True))
    spread = lax.optimization_barrier(jnp.mean(centre * centre, axis=-1, keepdims=True))
    return centre * lax.rsqrt(spread + epsilon) * gain_vec

def matmul(left, right):
    return jnp.dot(left, right, precision=lax.Precision.HIGHEST, preferred_element_type=jnp.float32)

def multiplicity(query_at, key_at, offsets):
    seg_spans = (SEGMENT, 2 * SEGMENT, 4 * SEGMENT, 8 * SEGMENT)
    segment_dilation_rates = (1, DILATION_SECOND, DILATION_THIRD, DILATION_FOURTH)
    counted = jnp.zeros((offsets.shape[1], query_at.shape[0], key_at.shape[0]), jnp.float32)
    for branch in range(4):
        seg_span = seg_spans[branch]
        seg_rate = segment_dilation_rates[branch]
        same_seg = query_at[:, None] // seg_span == key_at[None, :] // seg_span
        query_hit = (query_at % seg_span % seg_rate)[None, :] == offsets[branch][:, None]
        key_hit = (key_at % seg_span % seg_rate)[None, :] == offsets[branch][:, None]
        joined = same_seg[None, :, :] & query_hit[:, :, None] & key_hit[:, None, :]
        counted = counted + joined.astype(jnp.float32)
    causal = key_at[None, :] // BLOCK <= query_at[:, None] // BLOCK
    return jnp.where(causal[None, :, :], counted, 0.0)

def attend(query_rows, key_rows, value_rows, offsets):
    seq_len = query_rows.shape[0]
    row_tile = min(512, seq_len)
    key_pos = jnp.arange(seq_len, dtype=jnp.int32)
    inv_root = 1.0 / math.sqrt(HEAD_DIM)

    def one_tile(tile_idx):
        row_start = tile_idx * row_tile
        query_part = lax.dynamic_slice_in_dim(query_rows, row_start, row_tile, 0)
        query_pos = row_start + jnp.arange(row_tile, dtype=jnp.int32)
        scores = jnp.einsum('qhe,khe->hqk', query_part, key_rows, precision=lax.Precision.HIGHEST) * inv_root
        scores = low_back(scores)
        counts = multiplicity(query_pos, key_pos, offsets)
        logits = jnp.where(counts > 0, scores + jnp.log(jnp.maximum(counts, 1.0)), -jnp.inf)
        row_max = lax.optimization_barrier(jnp.max(logits, axis=-1, keepdims=True))
        exp_terms = jnp.exp(logits - row_max)
        attn_probs = exp_terms / lax.optimization_barrier(jnp.sum(exp_terms, axis=-1, keepdims=True))
        return jnp.einsum('hqk,khe->qhe', low(attn_probs), value_rows, precision=lax.Precision.HIGHEST)
    row_tiles = lax.map(jax.checkpoint(one_tile), jnp.arange(seq_len // row_tile, dtype=jnp.int32))
    return row_tiles.reshape(seq_len, HEADS * HEAD_DIM)

def layer_forward(seq_rows, params, offsets):
    w_qkv, b_query, b_value, w_out, b_out, w_in, b_in, w_down, b_down, gain_pre, gain_attn, gain_ffn_pre, gain_ffn_mid = params
    seq_len = seq_rows.shape[0]
    normed_in = low(layer_norm(seq_rows, gain_pre))
    projected = matmul(normed_in, w_qkv)
    queries = low_back(low(projected[:, :D] + b_query))
    key_rows = low_back(low(projected[:, D:2 * D]))
    value_rows = low_back(low(projected[:, 2 * D:] + b_value))
    attended = attend(queries.reshape(seq_len, HEADS, HEAD_DIM), key_rows.reshape(seq_len, HEADS, HEAD_DIM), value_rows.reshape(seq_len, HEADS, HEAD_DIM), offsets)
    attended = low_back(low(attended))
    normed_att = low(layer_norm(attended, gain_attn))
    middle = seq_rows + low_back(matmul(normed_att, w_out) + b_out)
    normed_mid = low(layer_norm(middle, gain_ffn_pre))
    pre_act = low_back(matmul(normed_mid, w_in) + b_in)
    inner_out = low(layer_norm(jax.nn.gelu(pre_act, approximate=False), gain_ffn_mid))
    return middle + low_back(matmul(inner_out, w_down) + b_down)

def reference(inputs, cotangent, head_offsets, w_qkv, b_query, b_value, w_out, b_out, w_in, b_in, w_down, b_down, gain_pre, gain_attn, gain_ffn_pre, gain_ffn_mid):
    params = (w_qkv.astype(jnp.float32), b_query.astype(jnp.float32), b_value.astype(jnp.float32), w_out.astype(jnp.float32), b_out.astype(jnp.float32), w_in.astype(jnp.float32), b_in.astype(jnp.float32), w_down.astype(jnp.float32), b_down.astype(jnp.float32), gain_pre.astype(jnp.float32), gain_attn.astype(jnp.float32), gain_ffn_pre.astype(jnp.float32), gain_ffn_mid.astype(jnp.float32))

    def one_sequence(totals, seq_pair):
        seq_in, seq_cot = seq_pair

        def forward(seq_rows, weights):
            return layer_forward(seq_rows, weights, head_offsets)
        result, pullback = jax.vjp(forward, seq_in, params)
        grad_x, grad_params = pullback(seq_cot)
        totals = jax.tree.map(jnp.add, totals, grad_params)
        return (totals, (result, grad_x))
    zero_grads = jax.tree.map(jnp.zeros_like, params)
    totals, (outputs, grad_inputs) = lax.scan(one_sequence, zero_grads, (inputs, cotangent))
    return (outputs, grad_inputs, totals[0], totals[1], totals[2], totals[3], totals[4], totals[5], totals[6], totals[7], totals[8], totals[9], totals[10], totals[11], totals[12])
```

```python
import functools
import math

import jax
import jax.numpy as jnp
from jax import lax
from jax.experimental import pallas as pl
from jax.experimental.pallas import tpu as pltpu
from jax.sharding import PartitionSpec as P

D = 768
HEADS = 12
HEAD_DIM = 64
SEGMENT = 2048
BLOCK = 256
DILATION_SECOND = 2
DILATION_THIRD = 4
DILATION_FOURTH = 6


epsilon = 1e-05
negative = -1e30


def layer_norm(values, gain_vec):
    centre = values - jnp.mean(values, axis=-1, keepdims=True)
    spread = jnp.mean(centre * centre, axis=-1, keepdims=True)
    return centre * lax.rsqrt(spread + epsilon) * gain_vec


def feature_norm(values, gain_vec):
    centre = values - jnp.mean(values, axis=0, keepdims=True)
    spread = jnp.mean(centre * centre, axis=0, keepdims=True)
    return centre * lax.rsqrt(spread + epsilon) * gain_vec[:, None, None]


def gelu_norm(values, gain_vec):
    return layer_norm(jax.nn.gelu(values, approximate=False), gain_vec)


def multiplicity(query_at, key_at, offsets):
    seg_spans = (SEGMENT, 2 * SEGMENT, 4 * SEGMENT, 8 * SEGMENT)
    segment_dilation_rates = (1, DILATION_SECOND, DILATION_THIRD, DILATION_FOURTH)
    counted = jnp.zeros((offsets.shape[1], query_at.shape[0], key_at.shape[0]), jnp.float32)
    for branch in range(4):
        seg_span = seg_spans[branch]
        seg_rate = segment_dilation_rates[branch]
        same_seg = query_at[:, None] // seg_span == key_at[None, :] // seg_span
        query_hit = (query_at % seg_span % seg_rate)[None, :] == offsets[branch][:, None]
        key_hit = (key_at % seg_span % seg_rate)[None, :] == offsets[branch][:, None]
        joined = same_seg[None, :, :] & query_hit[:, :, None] & key_hit[:, None, :]
        counted = counted + joined.astype(jnp.float32)
    causal = key_at[None, :] // BLOCK <= query_at[:, None] // BLOCK
    return jnp.where(causal[None, :, :], counted, 0.0)


def tile_loop(outer_count, inner_count, tile_step, initial):

    def outer_step(outer_idx, outer_state):

        def inner_step(inner_idx, inner_state):
            return tile_step(outer_idx, inner_idx, inner_state)

        return lax.fori_loop(0, inner_count, inner_step, outer_state)

    return lax.fori_loop(0, outer_count, outer_step, initial)


def online_step(previous, logits, valid, value_blk, query_first, query_tile):
    run_max, run_sum, run_acc = previous
    old_max = lax.dynamic_slice_in_dim(run_max, query_first, query_tile, 2)
    new_max = jnp.maximum(old_max, jnp.max(logits, axis=-1))
    exp_terms = jnp.where(valid, jnp.exp(logits - new_max[..., None]), 0.0)
    rescale = jnp.exp(old_max - new_max)
    old_sum = lax.dynamic_slice_in_dim(run_sum, query_first, query_tile, 2)
    new_sum = old_sum * rescale + jnp.sum(exp_terms, axis=-1)
    old_acc = lax.dynamic_slice_in_dim(run_acc, query_first, query_tile, 3)
    weighted = jnp.einsum(
        "hsqk,hesk->hesq",
        exp_terms.astype(jnp.bfloat16),
        value_blk,
        preferred_element_type=jnp.float32,
    )
    new_acc = old_acc * rescale[:, None] + weighted
    return (
        lax.dynamic_update_slice_in_dim(run_max, new_max, query_first, 2),
        lax.dynamic_update_slice_in_dim(run_sum, new_sum, query_first, 2),
        lax.dynamic_update_slice_in_dim(run_acc, new_acc, query_first, 3),
    )


def general_device(
    inputs,
    cotangent,
    head_offsets,
    w_qkv,
    b_query,
    b_value,
    w_out,
    b_out,
    w_in,
    b_in,
    w_down,
    b_down,
    gain_pre,
    gain_attn,
    gain_ffn_pre,
    gain_ffn_mid,
):
    gathered = (
        lax.all_gather(w_qkv, ("dp", "ctx", "head"), axis=0, tiled=True),
        lax.all_gather(b_query, ("dp", "ctx", "head"), axis=0, tiled=True),
        lax.all_gather(b_value, ("dp", "ctx", "head"), axis=0, tiled=True),
        lax.all_gather(w_out, ("dp", "ctx", "head"), axis=0, tiled=True),
        lax.all_gather(b_out, ("dp", "ctx", "head"), axis=0, tiled=True),
        lax.all_gather(w_in, ("dp", "ctx", "head"), axis=0, tiled=True),
        lax.all_gather(b_in, ("dp", "ctx", "head"), axis=0, tiled=True),
        lax.all_gather(w_down, ("dp", "ctx", "head"), axis=0, tiled=True),
        lax.all_gather(b_down, ("dp", "ctx", "head"), axis=0, tiled=True),
        lax.all_gather(gain_pre, ("dp", "ctx", "head"), axis=0, tiled=True),
        lax.all_gather(gain_attn, ("dp", "ctx", "head"), axis=0, tiled=True),
        lax.all_gather(gain_ffn_pre, ("dp", "ctx", "head"), axis=0, tiled=True),
        lax.all_gather(gain_ffn_mid, ("dp", "ctx", "head"), axis=0, tiled=True),
    )
    qkv_weight = gathered[0]
    query_bias = gathered[1].astype(jnp.float32)
    value_bias = gathered[2].astype(jnp.float32)
    out_weight = gathered[3]
    out_bias = gathered[4].astype(jnp.float32)
    in_weight = gathered[5]
    in_bias = gathered[6].astype(jnp.float32)
    down_weight = gathered[7]
    down_bias = gathered[8].astype(jnp.float32)
    pre_gain = gathered[9].astype(jnp.float32)
    attn_gain = gathered[10].astype(jnp.float32)
    ffn_gain = gathered[11].astype(jnp.float32)
    mid_gain = gathered[12].astype(jnp.float32)
    groups = lax.axis_size("head")
    per_group = HEADS // groups
    group_width = per_group * HEAD_DIM
    seq_count = inputs.shape[0]
    tok_count = inputs.shape[1]
    local_len = tok_count * groups
    inv_root = 1.0 / math.sqrt(HEAD_DIM)
    position = lax.axis_index("ctx")
    ctx_first = position * local_len
    own_offsets = lax.dynamic_slice_in_dim(
        head_offsets, lax.axis_index("head") * per_group, per_group, 1
    )
    query_tile = math.gcd(local_len, 512)
    query_tiles = local_len // query_tile
    normed_in, pre_pull = jax.vjp(layer_norm, inputs, pre_gain)
    in_low = normed_in.astype(jnp.bfloat16)
    projected = lax.dot_general(
        qkv_weight, in_low, (((0,), (2,)), ((), ())), preferred_element_type=jnp.float32
    )
    bias_cols = jnp.concatenate([query_bias, jnp.zeros_like(query_bias), value_bias])
    qkv_low = (projected + bias_cols[:, None, None]).astype(jnp.bfloat16)
    qkv_low = qkv_low.reshape(3, groups, group_width, seq_count, tok_count)
    regrouped = lax.all_to_all(qkv_low, "head", split_axis=1, concat_axis=4, tiled=True)
    regrouped = regrouped.reshape(3, per_group, HEAD_DIM, seq_count, local_len)
    heads_of_query = regrouped[0]
    key_heads = regrouped[1]
    value_heads = regrouped[2]

    def tile_logits(query_blk, key_blk, query_at, key_at):
        scores = (
            jnp.einsum("hesq,hesk->hsqk", query_blk, key_blk, preferred_element_type=jnp.float32)
            * inv_root
        )
        counts = multiplicity(query_at, key_at, own_offsets)[:, None]
        logits = jnp.where(counts > 0, scores + jnp.log(jnp.maximum(counts, 1.0)), negative)
        return (logits, counts)

    def tile_probs(query_blk, key_blk, query_at, key_at, lse_blk):
        logits, counts = tile_logits(query_blk, key_blk, query_at, key_at)
        return jnp.where(counts > 0, jnp.exp(logits - lse_blk[..., None]), 0.0)

    start_max = jnp.full((per_group, seq_count, local_len), negative, jnp.float32)
    zero_sum = jnp.zeros((per_group, seq_count, local_len), jnp.float32)
    zero_acc = jnp.zeros((per_group, HEAD_DIM, seq_count, local_len), jnp.float32)
    key_piece = lax.all_gather(key_heads, "ctx", axis=3, tiled=True)
    value_piece = lax.all_gather(value_heads, "ctx", axis=3, tiled=True)
    key_tile = math.gcd(key_piece.shape[3], 512)

    def forward_one_tile(key_idx, query_idx, fold_state):
        key_first = key_idx * key_tile
        query_first = query_idx * query_tile
        key_at = key_first + jnp.arange(key_tile, dtype=jnp.int32)
        query_at = ctx_first + query_first + jnp.arange(query_tile, dtype=jnp.int32)

        def forward_update(previous):
            key_blk = lax.dynamic_slice_in_dim(key_piece, key_first, key_tile, 3)
            value_blk = lax.dynamic_slice_in_dim(value_piece, key_first, key_tile, 3)
            query_blk = lax.dynamic_slice_in_dim(heads_of_query, query_first, query_tile, 3)
            logits, counts = tile_logits(query_blk, key_blk, query_at, key_at)
            return online_step(previous, logits, counts > 0, value_blk, query_first, query_tile)

        beyond = key_at[0] // BLOCK > query_at[query_tile - 1] // BLOCK
        return lax.cond(beyond, lambda previous: previous, forward_update, fold_state)

    run_max, run_sum, run_acc = tile_loop(
        key_piece.shape[3] // key_tile,
        query_tiles,
        forward_one_tile,
        (start_max, zero_sum, zero_acc),
    )
    log_sums = run_max + jnp.log(run_sum)
    attended = run_acc / run_sum[:, None]
    out_low = attended.astype(jnp.bfloat16).reshape(1, group_width, seq_count, local_len)
    returned = lax.all_to_all(out_low, "head", split_axis=3, concat_axis=0, tiled=True)
    attn_in = returned.reshape(D, seq_count, tok_count).astype(jnp.float32)
    normed_att, attn_pull = jax.vjp(feature_norm, attn_in, attn_gain)
    att_low = normed_att.astype(jnp.bfloat16)
    branch_out = lax.dot_general(
        att_low, out_weight, (((0,), (0,)), ((), ())), preferred_element_type=jnp.float32
    )
    middle = inputs + branch_out + out_bias
    normed_mid, ffn_pull = jax.vjp(layer_norm, middle, ffn_gain)
    mid_low = normed_mid.astype(jnp.bfloat16)
    pre_act = jnp.dot(mid_low, in_weight, preferred_element_type=jnp.float32) + in_bias
    inner_out, gelu_pull = jax.vjp(gelu_norm, pre_act, mid_gain)
    inner_low = inner_out.astype(jnp.bfloat16)
    outputs = (
        middle + jnp.dot(inner_low, down_weight, preferred_element_type=jnp.float32) + down_bias
    )
    g_out = cotangent.astype(jnp.bfloat16)
    grad_down = lax.dot_general(
        inner_low, g_out, (((0, 1), (0, 1)), ((), ())), preferred_element_type=jnp.float32
    )
    down_bias_gradient = jnp.sum(g_out.astype(jnp.float32), axis=(0, 1))
    g_inner = lax.dot_general(
        g_out, down_weight, (((2,), (1,)), ((), ())), preferred_element_type=jnp.float32
    )
    g_pre, grad_mid_gain = gelu_pull(g_inner)
    pre_low = g_pre.astype(jnp.bfloat16)
    grad_in_bias = jnp.sum(pre_low.astype(jnp.float32), axis=(0, 1))
    grad_in = lax.dot_general(
        mid_low, pre_low, (((0, 1), (0, 1)), ((), ())), preferred_element_type=jnp.float32
    )
    g_normed_mid = lax.dot_general(
        pre_low, in_weight, (((2,), (1,)), ((), ())), preferred_element_type=jnp.float32
    )
    g_mid_part, grad_ffn_gain = ffn_pull(g_normed_mid)
    g_middle = cotangent + g_mid_part
    branch_gradient = g_middle.astype(jnp.bfloat16)
    grad_out_bias = jnp.sum(branch_gradient.astype(jnp.float32), axis=(0, 1))
    grad_out = lax.dot_general(
        att_low, branch_gradient, (((1, 2), (0, 1)), ((), ())), preferred_element_type=jnp.float32
    )
    normed_attention_gradient = lax.dot_general(
        out_weight, branch_gradient, (((1,), (2,)), ((), ())), preferred_element_type=jnp.float32
    )
    g_attn_in, grad_attn_gain = attn_pull(normed_attention_gradient)
    g_att_low = g_attn_in.astype(jnp.bfloat16).reshape(groups, group_width, seq_count, tok_count)
    g_heads = lax.all_to_all(g_att_low, "head", split_axis=0, concat_axis=3, tiled=True)
    g_heads = g_heads.reshape(per_group, HEAD_DIM, seq_count, local_len)
    delta = jnp.sum(g_heads.astype(jnp.float32) * attended, axis=1)
    query_key_piece = lax.all_gather(key_heads, "ctx", axis=3, tiled=True)
    query_value_piece = lax.all_gather(value_heads, "ctx", axis=3, tiled=True)
    query_key_tile = math.gcd(query_key_piece.shape[3], 512)

    def query_one_tile(key_idx, query_idx, grad_state):
        key_first = key_idx * query_key_tile
        query_first = query_idx * query_tile
        key_at = key_first + jnp.arange(query_key_tile, dtype=jnp.int32)
        query_at = ctx_first + query_first + jnp.arange(query_tile, dtype=jnp.int32)

        def query_update(previous):
            key_blk = lax.dynamic_slice_in_dim(query_key_piece, key_first, query_key_tile, 3)
            value_blk = lax.dynamic_slice_in_dim(query_value_piece, key_first, query_key_tile, 3)
            query_blk = lax.dynamic_slice_in_dim(heads_of_query, query_first, query_tile, 3)
            gout_blk = lax.dynamic_slice_in_dim(g_heads, query_first, query_tile, 3)
            lse_blk = lax.dynamic_slice_in_dim(log_sums, query_first, query_tile, 2)
            delta_blk = lax.dynamic_slice_in_dim(delta, query_first, query_tile, 2)
            tile_prob = tile_probs(query_blk, key_blk, query_at, key_at, lse_blk)
            g_probs = jnp.einsum(
                "hesq,hesk->hsqk", gout_blk, value_blk, preferred_element_type=jnp.float32
            )
            g_scores = (tile_prob * (g_probs - delta_blk[..., None])).astype(jnp.bfloat16)
            step_grad = (
                jnp.einsum("hsqk,hesk->hesq", g_scores, key_blk, preferred_element_type=jnp.float32)
                * inv_root
            )
            earlier = lax.dynamic_slice_in_dim(previous, query_first, query_tile, 3)
            return lax.dynamic_update_slice_in_dim(previous, earlier + step_grad, query_first, 3)

        beyond = key_at[0] // BLOCK > query_at[query_tile - 1] // BLOCK
        return lax.cond(beyond, lambda previous: previous, query_update, grad_state)

    grad_query = tile_loop(
        query_key_piece.shape[3] // query_key_tile, query_tiles, query_one_tile, zero_acc
    )
    all_lse, all_delta = (
        lax.all_gather(log_sums, "ctx", axis=2, tiled=True),
        lax.all_gather(delta, "ctx", axis=2, tiled=True),
    )
    query_piece = lax.all_gather(heads_of_query, "ctx", axis=3, tiled=True)
    gout_piece = lax.all_gather(g_heads, "ctx", axis=3, tiled=True)
    row_tile = math.gcd(query_piece.shape[3], 512)

    def key_one_tile(query_idx, key_idx, grad_state):
        query_first = query_idx * row_tile
        key_first = key_idx * query_tile
        query_at = query_first + jnp.arange(row_tile, dtype=jnp.int32)
        key_at = ctx_first + key_first + jnp.arange(query_tile, dtype=jnp.int32)

        def key_update(previous):
            key_sum, value_sum = previous
            query_blk = lax.dynamic_slice_in_dim(query_piece, query_first, row_tile, 3)
            gout_blk = lax.dynamic_slice_in_dim(gout_piece, query_first, row_tile, 3)
            lse_blk = lax.dynamic_slice_in_dim(all_lse, query_first, row_tile, 2)
            delta_blk = lax.dynamic_slice_in_dim(all_delta, query_first, row_tile, 2)
            key_blk = lax.dynamic_slice_in_dim(key_heads, key_first, query_tile, 3)
            value_blk = lax.dynamic_slice_in_dim(value_heads, key_first, query_tile, 3)
            tile_prob = tile_probs(query_blk, key_blk, query_at, key_at, lse_blk)
            value_step = jnp.einsum(
                "hsqk,hesq->hesk",
                tile_prob.astype(jnp.bfloat16),
                gout_blk,
                preferred_element_type=jnp.float32,
            )
            g_probs = jnp.einsum(
                "hesq,hesk->hsqk", gout_blk, value_blk, preferred_element_type=jnp.float32
            )
            g_scores = (tile_prob * (g_probs - delta_blk[..., None])).astype(jnp.bfloat16)
            key_step = (
                jnp.einsum(
                    "hsqk,hesq->hesk", g_scores, query_blk, preferred_element_type=jnp.float32
                )
                * inv_root
            )
            key_before = lax.dynamic_slice_in_dim(key_sum, key_first, query_tile, 3)
            value_before = lax.dynamic_slice_in_dim(value_sum, key_first, query_tile, 3)
            return (
                lax.dynamic_update_slice_in_dim(key_sum, key_before + key_step, key_first, 3),
                lax.dynamic_update_slice_in_dim(value_sum, value_before + value_step, key_first, 3),
            )

        beyond = key_at[0] // BLOCK > query_at[row_tile - 1] // BLOCK
        return lax.cond(beyond, lambda previous: previous, key_update, grad_state)

    grad_key, grad_value = tile_loop(
        query_piece.shape[3] // row_tile, query_tiles, key_one_tile, (zero_acc, zero_acc)
    )
    stacked = jnp.stack([grad_query, grad_key, grad_value]).astype(jnp.bfloat16)
    stacked = stacked.reshape(3, 1, group_width, seq_count, local_len)
    g_qkv = lax.all_to_all(stacked, "head", split_axis=4, concat_axis=1, tiled=True)
    g_qkv = g_qkv.reshape(3 * D, seq_count, tok_count)
    qkv_sums = jnp.sum(g_qkv.astype(jnp.float32), axis=(1, 2))
    grad_query_bias = qkv_sums[:D]
    grad_value_bias = qkv_sums[2 * D :]
    grad_qkv = lax.dot_general(
        in_low, g_qkv, (((0, 1), (1, 2)), ((), ())), preferred_element_type=jnp.float32
    )
    g_normed_in = lax.dot_general(
        g_qkv, qkv_weight, (((0,), (1,)), ((), ())), preferred_element_type=jnp.float32
    )
    g_in_part, grad_pre_gain = pre_pull(g_normed_in)
    grad_inputs = g_middle + g_in_part
    reduced = (
        lax.psum_scatter(grad_qkv, ("dp", "ctx", "head"), scatter_dimension=0, tiled=True),
        lax.psum_scatter(grad_query_bias, ("dp", "ctx", "head"), scatter_dimension=0, tiled=True),
        lax.psum_scatter(grad_value_bias, ("dp", "ctx", "head"), scatter_dimension=0, tiled=True),
        lax.psum_scatter(grad_out, ("dp", "ctx", "head"), scatter_dimension=0, tiled=True),
        lax.psum_scatter(grad_out_bias, ("dp", "ctx", "head"), scatter_dimension=0, tiled=True),
        lax.psum_scatter(grad_in, ("dp", "ctx", "head"), scatter_dimension=0, tiled=True),
        lax.psum_scatter(grad_in_bias, ("dp", "ctx", "head"), scatter_dimension=0, tiled=True),
        lax.psum_scatter(grad_down, ("dp", "ctx", "head"), scatter_dimension=0, tiled=True),
        lax.psum_scatter(
            down_bias_gradient, ("dp", "ctx", "head"), scatter_dimension=0, tiled=True
        ),
        lax.psum_scatter(grad_pre_gain, ("dp", "ctx", "head"), scatter_dimension=0, tiled=True),
        lax.psum_scatter(grad_attn_gain, ("dp", "ctx", "head"), scatter_dimension=0, tiled=True),
        lax.psum_scatter(grad_ffn_gain, ("dp", "ctx", "head"), scatter_dimension=0, tiled=True),
        lax.psum_scatter(grad_mid_gain, ("dp", "ctx", "head"), scatter_dimension=0, tiled=True),
    )
    return (
        outputs,
        grad_inputs,
        reduced[0],
        reduced[1],
        reduced[2],
        reduced[3],
        reduced[4],
        reduced[5],
        reduced[6],
        reduced[7],
        reduced[8],
        reduced[9],
        reduced[10],
        reduced[11],
        reduced[12],
    )


F32 = jnp.float32
LOW = jnp.bfloat16
MESH = pl.DeviceIdType.MESH
TOK = 256
WIDE = 768
LANES = 256
PARTS = 4
CORES = 2
GROUPS = 4
SLABS = 32
SUB = 24
QKV_ROWS = 32
BIG_ROWS = 224
PIECE = 112


def dot_nn(left, right):
    return lax.dot_general(left, right, (((1,), (0,)), ((), ())), preferred_element_type=F32)


def dot_nt(left, right):
    return lax.dot_general(left, right, (((1,), (1,)), ((), ())), preferred_element_type=F32)


def dot_tn(left, right):
    return lax.dot_general(left, right, (((0,), (0,)), ((), ())), preferred_element_type=F32)


def iota(shape, axis):
    return lax.broadcasted_iota(jnp.int32, shape, axis)


def row_mean(values):
    return jnp.mean(values, axis=-1, keepdims=True)


def spread_vector(rows, row, first, piece, width):
    select = (iota((128, width), 0) == lax.rem(iota((128, width), 1), piece)).astype(LOW)
    spread = dot_nn(rows, select)
    at = iota((SLABS * 8, width), 0)
    want = (first + iota((SLABS * 8, width), 1) // piece) * 8 + row
    return jnp.sum(jnp.where(at == want, spread, 0.0), axis=0, keepdims=True)


def slab_rows(vectors, first, piece, width):
    wide = jnp.broadcast_to(vectors[None], (SLABS, 8, width)).reshape(SLABS * 8, width)
    mine = first + iota((SLABS * 8, width), 1) // piece == iota((SLABS * 8, width), 0) // 8
    select = (iota((128, width), 0) == lax.rem(iota((128, width), 1), piece)).astype(LOW)
    return dot_nt(jnp.where(mine, wide, 0.0).astype(LOW), select)


class Place:
    def __init__(self):
        self.dp = lax.axis_index("dp")
        self.c = lax.axis_index("ctx")
        self.h = lax.axis_index("head")
        self.x = lax.rem(self.dp, 2)
        self.y = self.dp // 2
        self.xn = self.dp + 1 - 2 * self.x
        self.yn = self.dp + 2 - 4 * self.y
        self.cn = 1 - self.c

    def z(self, k):
        return lax.rem(self.h + k, GROUPS)

    def z_from(self, k):
        return lax.rem(self.h + GROUPS - k, GROUPS)

    def q_block(self, i):
        first = (0, 3, 4, 7)[i]
        second = (1, 2, 5, 6)[i]
        return first + (second - first) * self.c

    def core_of(self, block):
        low = lax.rem(block, 4)
        return jnp.where((low == 0) | (low == 3), 0, 1)


def enter(place):
    barrier = pltpu.get_barrier_semaphore()
    peers = [{"ctx": o, "head": place.z(k)} for k in range(GROUPS) for o in (place.c, place.cn)][1:]
    peers += [{"dp": place.xn}, {"dp": place.yn}]
    for peer in peers:
        pl.semaphore_signal(barrier, inc=1, device_id=peer, device_id_type=MESH)
    pl.semaphore_wait(barrier, len(peers))


def remote(src, dst, send, recv, peer):
    return pltpu.make_async_remote_copy(
        src_ref=src, dst_ref=dst, send_sem=send, recv_sem=recv, device_id=peer, device_id_type=MESH
    )


def count_tables(offs_ref, now_ref, group, query, keys_first, base=0, count=8):
    @pl.loop(0, 3)
    def _(j):
        for b in range(3):
            start = (TOK * b, TOK * lax.rem(query, 3))
            row_start, col_start = start if keys_first else start[::-1]
            rows = iota((TOK, 1), 0) + row_start
            cols = iota((1, TOK), 1) + col_start
            total = jnp.ones((TOK, TOK), F32)
            for branch, rate in ((1, DILATION_SECOND), (2, DILATION_THIRD), (3, DILATION_FOURTH)):
                offset = offs_ref[branch, group * 3 + j]
                row_hit = jnp.where(lax.rem(rows, rate) == offset, 1.0, 0.0)
                col_hit = jnp.where(lax.rem(cols, rate) == offset, 1.0, 0.0)
                total = total + row_hit * col_hit
            for key in range(b, count, 3):
                now_ref[j, base + key] = total


def head_masks():
    lane = iota((TOK, 128), 1)
    return lane < 64, lane >= 64


def split_heads(both):
    low, high = head_masks()
    zero = jnp.zeros((TOK, 128), both.dtype)
    return (
        jnp.where(low, both[:, :128], zero),
        jnp.where(high, both[:, :128], zero),
        both[:, 128:],
    )


def nearby(place, step):
    return ((place.h >= step, place.h - step, True), (place.h + step < GROUPS, place.h + step, False))


def z_relay(place, view, item, up, sems):
    to = lax.rem(place.h + (1 if up else GROUPS - 1), GROUPS)
    more = place.h < GROUPS - 1 if up else place.h > 0
    return more, remote(view(item), view(item), sems[0 if up else 1].at[item], sems[2].at[item], {"head": to})


def pack_third(third):
    half = TOK // 2
    return jnp.where(iota((half, 128), 1) < 64, third[:half], pltpu.roll(third[half:], 64, 1))


def unpack_third(packed):
    return jnp.concatenate([packed, pltpu.roll(packed, 64, 1)], axis=0)


class Gather:
    def __init__(self, place, big_ref, sems, first):
        self.p, self.big, self.sems = place, big_ref, sems
        self.z_sems = sems[0:3]
        half = PIECE // 2
        self.rows, self.one, self.two = pl.ds(first, PIECE), pl.ds(first, half), pl.ds(first + half, half)

    def z_view(self, item):
        return self.big.at[self.p.dp, self.p.c, item, self.rows]

    def copy(self, src, item, kind, peer):
        return remote(src, src, self.sems[3 + 2 * kind].at[item], self.sems[4 + 2 * kind].at[item], peer)

    def x_copy(self, item):
        return self.copy(self.z_view(item), item, 0, {"dp": self.p.xn})

    def y_copy(self, item):
        return self.copy(self.z_view(item), item, 1, {"dp": self.p.yn})

    def to_y(self, item):
        return self.copy(self.big.at[self.p.xn, self.p.c, item, self.one], item, 2, {"dp": self.p.yn})

    def to_x(self, item):
        return self.copy(self.big.at[self.p.yn, self.p.c, item, self.two], item, 3, {"dp": self.p.xn})

    def core_copy(self, item):
        return self.copy(self.big.at[:, self.p.c, item, self.rows], item, 4, {"ctx": self.p.cn})

    def own_xy(self):
        self.x_copy(self.p.h).start()
        self.y_copy(self.p.h).start()

    def own_z(self):
        for up in (True, False):
            more, copy = z_relay(self.p, self.z_view, self.p.h, up, self.z_sems)
            pl.when(more)(copy.start)

    def items(self, step):
        return nearby(self.p, step) if step else ((self.p.h >= 0, self.p.h, True),)

    def arrive(self, step):
        for there, item, up in self.items(step):

            @pl.when(there)
            def _():
                more, copy = z_relay(self.p, self.z_view, item, up, self.z_sems)
                copy.wait_recv()
                pl.when(more)(copy.start)
                self.x_copy(item).start()
                self.y_copy(item).start()

    def forward(self, step):
        for there, item, _ in self.items(step):

            @pl.when(there)
            def _():
                self.x_copy(item).wait_recv()
                self.to_y(item).start()
                self.y_copy(item).wait_recv()
                self.to_x(item).start()

    def across(self, step):
        for there, item, _ in self.items(step):

            @pl.when(there)
            def _():
                self.to_y(item).wait_recv()
                self.to_x(item).wait_recv()
                self.core_copy(item).start()

    def finish(self):
        for step in range(GROUPS):
            for there, item, up in self.items(step):

                @pl.when(there)
                def _():
                    self.core_copy(item).wait()
                    for copy in (self.x_copy(item), self.y_copy(item), self.to_x(item), self.to_y(item)):
                        copy.wait_send()
                    for way in (True, False) if step == 0 else (up,):
                        more, copy = z_relay(self.p, self.z_view, item, way, self.z_sems)
                        pl.when(more)(copy.wait_send)


def column(row, size):
    same = iota((size, size), 0) == iota((size, size), 1)
    return jnp.sum(jnp.where(same, row, 0.0), axis=1, keepdims=True)


def flat(col, size):
    same = iota((size, size), 0) == iota((size, size), 1)
    return jnp.sum(jnp.where(same, col, 0.0), axis=0, keepdims=True)


def prepare(wqkv_ref, wout_ref, win_ref, wdown_ref, gains, biases, wq_ref, wb_ref, tmp_ref):
    pre, attn, ffn, mid = [
        column(gain[...].astype(F32), size) for gain, size in zip(gains, (SUB, SUB, SUB, 4 * SUB))
    ]
    b_query, b_value, b_out, b_in, b_down = biases
    for part in range(3):
        scaled = wqkv_ref[:, part * WIDE : (part + 1) * WIDE].astype(F32) * pre
        for group in range(GROUPS):
            turned = pltpu.roll(scaled, (WIDE - 192 * group) % WIDE, 1) if group else scaled
            piece = jnp.where(iota((SUB, LANES), 1) < 192, turned[:, :LANES], 0.0)
            wq_ref[group, :SUB, part * LANES : (part + 1) * LANES] = piece.astype(LOW)
    tmp_ref[...] = jnp.zeros_like(tmp_ref)
    tmp_ref[0:1, :SUB] = b_query[...].astype(F32)
    tmp_ref[1:2, :SUB] = b_value[...].astype(F32)
    small = tmp_ref[...].astype(LOW)
    for group in range(GROUPS):
        wq_ref[group, SUB:, :] = small
    wb_ref[0:SUB, :] = (wout_ref[...].astype(F32) * attn).astype(LOW)
    for m in range(4):
        cols = win_ref[:, m * WIDE : (m + 1) * WIDE].astype(F32) * ffn
        wb_ref[SUB + SUB * m : 2 * SUB + SUB * m, :] = cols.astype(LOW)
    wb_ref[120:216, :] = (wdown_ref[...].astype(F32) * mid).astype(LOW)
    tmp_ref[0:1, :SUB] = b_out[...].astype(F32)
    tmp_ref[1:2, :SUB] = b_down[...].astype(F32)
    tmp_ref[2:3, : 4 * SUB] = b_in[...].astype(F32)
    wb_ref[216:, :] = tmp_ref[...].astype(LOW)


def finish_kernel(
    x_ref, gmid_ref, back_ref, rs_ref, rq_ref, wqkv_ref, wout_ref, win_ref, wdown_ref, gains_refs,
    gx_ref, grads_refs, vectors_refs,
):
    back = back_ref[...]
    rows = x_ref[...]
    centre = rows - row_mean(rows)
    scale = lax.rsqrt(row_mean(centre * centre) + epsilon)
    normed = centre * scale
    gx_ref[...] = gmid_ref[...] + scale * (back - row_mean(back) - normed * row_mean(back * normed))
    pre, attn, ffn, mid = [
        column(gain[...].astype(F32), size) for gain, size in zip(gains_refs, (SUB, SUB, SUB, 4 * SUB))
    ]
    g_qkv, g_out, g_in, g_down = grads_refs
    v_query, v_value, v_out, v_in, v_down, v_pre, v_attn, v_ffn, v_mid = vectors_refs
    total = jnp.zeros((SUB, 1), F32)
    for part in range(3):
        raw = jnp.zeros((SUB, WIDE), F32)
        for group in range(GROUPS):
            piece = rq_ref[group, :SUB, part * LANES : (part + 1) * LANES]
            wide = jnp.concatenate([piece, jnp.zeros((SUB, WIDE - LANES), F32)], axis=1)
            raw = raw + (pltpu.roll(wide, 192 * group, 1) if group else wide)
        cols = slice(part * WIDE, (part + 1) * WIDE)
        g_qkv[:, cols] = pre * raw
        total = total + jnp.sum(wqkv_ref[:, cols].astype(F32) * raw, axis=1, keepdims=True)
    v_pre[...] = flat(total, SUB)
    small = rq_ref[0, SUB:, :128]
    for group in range(1, GROUPS):
        small = small + rq_ref[group, SUB:, :128]
    v_query[...] = small[0:1, :SUB]
    v_value[...] = small[1:2, :SUB]
    raw = rs_ref[0:SUB, :]
    g_out[...] = attn * raw
    v_attn[...] = flat(jnp.sum(wout_ref[...].astype(F32) * raw, axis=1, keepdims=True), SUB)
    total = jnp.zeros((SUB, 1), F32)
    for m in range(4):
        raw = rs_ref[SUB + SUB * m : 2 * SUB + SUB * m, :]
        cols = slice(m * WIDE, (m + 1) * WIDE)
        g_in[:, cols] = ffn * raw
        total = total + jnp.sum(win_ref[:, cols].astype(F32) * raw, axis=1, keepdims=True)
    v_ffn[...] = flat(total, SUB)
    raw = rs_ref[120:216, :]
    g_down[...] = mid * raw
    v_mid[...] = flat(jnp.sum(wdown_ref[...].astype(F32) * raw, axis=1, keepdims=True), 4 * SUB)
    small = rs_ref[216:, :128]
    v_out[...] = small[0:1, :SUB]
    v_down[...] = small[1:2, :SUB]
    v_in[...] = small[2:3, : 4 * SUB]


def forward_kernel(
    offs_ref, x_ref, wqkv_ref, wout_ref, win_ref, wdown_ref, gains_refs, bias_refs,
    xall_out, qkv_out, wg_out, big_ref, o_ref, lse_ref, att_ref,
    op_ref, xall_ref, qkv_ref, wg_ref, save_sem, wq_ref, wb_ref, tmp_ref, now_ref, score_ref, top_ref, acc_ref, wcat_ref, own_sem,
    nu, nd, nr, fs, fr, ws, wr, ats, atr, *big_sems,
):
    place = Place()
    dp, c, h = place.dp, place.c, place.h
    own = c * GROUPS + h
    n_sems = (nu, nd, nr)
    prepare(wqkv_ref, wout_ref, win_ref, wdown_ref, gains_refs, bias_refs, wq_ref, wb_ref, tmp_ref)
    own_copy = pltpu.make_async_copy(wb_ref, big_ref.at[dp, c, h], own_sem)
    own_copy.start()
    wg_ref[dp, c, h] = wq_ref[h]
    rows = x_ref[...]
    centre = rows - row_mean(rows)
    scale = lax.rsqrt(row_mean(centre * centre) + epsilon)
    xall_ref[own] = (centre * scale).astype(LOW)
    enter(place)

    def n_view(item):
        return xall_ref.at[c * GROUPS + item]

    def n_core(item):
        return remote(n_view(item), n_view(item), fs.at[item], fr.at[item], {"ctx": place.cn})

    for up in (True, False):
        more, copy = z_relay(place, n_view, h, up, n_sems)
        pl.when(more)(copy.start)
    n_core(h).start()
    wq_z = []
    for k in (1, 2, 3):
        copy = remote(wq_ref.at[place.z(k)], wg_ref.at[dp, c, h], ws.at[k - 1], wr.at[k - 1], {"head": place.z(k)})
        copy.start()
        wq_z.append(copy)
    own_copy.wait()
    gathers = [
        Gather(place, big_ref, big_sems[at * GATHER_SEMS : (at + 1) * GATHER_SEMS], first)
        for at, first in enumerate(range(0, BIG_ROWS, PIECE))
    ]

    def steps(name, *step):
        for gather in gathers:
            getattr(gather, name)(*step)

    steps("own_xy")
    two_dp = pl.ds(2 * place.y, 2)
    wq_x = remote(wg_ref.at[dp, c], wg_ref.at[dp, c], ws.at[3], wr.at[3], {"dp": place.xn})
    wq_y = remote(wg_ref.at[two_dp, c], wg_ref.at[two_dp, c], ws.at[4], wr.at[4], {"dp": place.yn})
    wq_c = remote(wg_ref.at[:, c], wg_ref.at[:, c], ws.at[5], wr.at[5], {"ctx": place.cn})

    def n_arrive(step):
        for there, item, up in nearby(place, step):

            @pl.when(there)
            def _():
                more, copy = z_relay(place, n_view, item, up, n_sems)
                copy.wait_recv()
                pl.when(more)(copy.start)
                n_core(item).start()

    for copy in wq_z:
        copy.wait()
    wq_x.start()
    for i in range(PARTS):
        count_tables(offs_ref, now_ref, h, place.q_block(i), False, i * (i + 1), 2 * i + 2)
    n_arrive(1)
    wq_x.wait()
    wq_y.start()
    n_arrive(2)
    steps("own_z")
    wq_y.wait()
    wq_c.start()
    steps("forward", 0)
    n_arrive(3)
    steps("across", 0)
    steps("arrive", 1)
    wq_c.wait()
    wcat_ref[...] = wg_ref[:, :, :, :SUB, :].reshape(WIDE, WIDE)
    small = wg_ref[:, :, :, SUB:, :128].reshape(SLABS * 8, 128)
    used = iota((1, LANES), 1) < 192
    bias_q = jnp.where(used, spread_vector(small, 0, 8 * h, SUB, LANES), 0.0)
    bias_v = jnp.where(used, spread_vector(small, 1, 8 * h, SUB, LANES), 0.0)
    for item in range(GROUPS):
        n_core(item).wait()
    for step in range(GROUPS):
        for there, item, up in gathers[0].items(step):
            for way in (True, False) if step == 0 else (up,):
                more, copy = z_relay(place, n_view, item, way, n_sems)
                pl.when(jnp.logical_and(there, more))(copy.wait_send)

    @pl.loop(0, 8)
    def _(block):
        both = dot_nn(xall_ref[block], wcat_ref[...])
        qkv_ref[block, :, :LANES] = ((both[:, :LANES] + bias_q).astype(LOW) * 0.125).astype(LOW)
        qkv_ref[block, :, LANES : 2 * LANES] = both[:, LANES : 2 * LANES].astype(LOW)
        qkv_ref[block, :, 2 * LANES :] = (both[:, 2 * LANES :] + bias_v).astype(LOW)

    saves = [
        pltpu.make_async_copy(src, dst, save_sem.at[at])
        for at, (src, dst) in enumerate(((xall_ref, xall_out), (qkv_ref, qkv_out), (wg_ref, wg_out)))
    ]
    for copy in saves:
        copy.start()
    sent = []
    for i in range(PARTS):
        block = place.q_block(i)
        queries = split_heads(qkv_ref[block, :, :LANES])

        top_ref[...] = jnp.full_like(top_ref, negative)
        acc_ref[...] = jnp.zeros_like(acc_ref)

        @pl.loop(0, 2 * i + 2)
        def _(key):
            @pl.when(key <= block)
            def _():
                keys = qkv_ref[key, :, LANES : 2 * LANES]
                for j in range(3):
                    scores = dot_nt(queries[j], keys[:, :128] if j < 2 else keys[:, 128:])
                    score_ref[j, key] = scores
                    top_ref[j] = jnp.maximum(top_ref[j], scores)

        tops = [jnp.max(top_ref[j], axis=1, keepdims=True) for j in range(3)]
        top_ref[...] = jnp.zeros_like(top_ref)

        @pl.loop(0, 2 * i + 2)
        def _(key):
            @pl.when(key <= block)
            def _():
                values = qkv_ref[key, :, 2 * LANES :]
                for j in range(3):
                    terms = jnp.exp(score_ref[j, key] - tops[j]) * now_ref[j, i * (i + 1) + key]
                    top_ref[j] += terms
                    acc_ref[j] += dot_nn(terms.astype(LOW), values[:, :128] if j < 2 else values[:, 128:])

        heads = []
        for j in range(3):
            total = jnp.sum(top_ref[j], axis=1, keepdims=True)
            heads.append(acc_ref[j] * (1.0 / total))
            column = jnp.broadcast_to(tops[j] + jnp.log(total), (TOK, 128))
            lse_ref[i, j] = column.T[:8]
        low, _ = head_masks()
        pair = jnp.where(low, heads[0], heads[1]).astype(LOW)
        o_ref[i, :, :128] = pair
        o_ref[i, :, 128:] = heads[2].astype(LOW)
        op_ref[i, :TOK] = pair
        op_ref[i, TOK:] = pack_third(heads[2]).astype(LOW)
        owner_c, owner_h = block // GROUPS, lax.rem(block, GROUPS)
        away = jnp.logical_or(owner_c != c, owner_h != h)
        copy = remote(op_ref.at[i], att_ref.at[h], ats.at[i], atr.at[h], {"ctx": owner_c, "head": owner_h})
        sent.append((away, copy))
        pl.when(away)(copy.start)

        @pl.when(jnp.logical_not(away))
        def _():
            att_ref[h] = op_ref[i]

        if i == 1:
            steps("arrive", 2)
            steps("forward", 1)
        if i == 2:
            steps("arrive", 3)

    steps("forward", 2)
    steps("across", 1)
    for away, copy in sent:
        pl.when(away)(copy.wait_send)
    for part in range(GROUPS):
        local = jnp.logical_and(h == part, place.core_of(own) == c)
        copy = remote(op_ref.at[0], att_ref.at[part], ats.at[0], atr.at[part], {"ctx": place.cn})
        pl.when(jnp.logical_not(local))(copy.wait_recv)
    steps("forward", 3)
    steps("across", 2)
    steps("across", 3)
    steps("finish")
    for copy in saves:
        copy.wait()


GATHER_SEMS = 13


def middle_kernel(
    x_ref, cot_ref, att_ref, big_in,
    out_ref, gmid_ref, gatt_ref, grad_out,
    big_ref, grad_ref, pre_ref, act_ref, gin_ref, wide_ref, load_sem, store_sem, down_sem,
):
    bounds = ((216, 224), (0, 24), (24, 120), (120, 216))

    def piece(src, dst, sem, first, last):
        rows = pl.ds(first, last - first)
        return pltpu.make_async_copy(src.at[:, rows], dst.at[:, rows], sem)

    loads = [piece(big_in, big_ref, load_sem.at[at], *bound) for at, bound in enumerate(bounds)]
    stores = [piece(grad_ref, grad_out, store_sem.at[at], *bound) for at, bound in enumerate(bounds[:3])]
    for copy in loads:
        copy.start()

    def down_store(m):
        slabs = pl.ds(8 * m, 8)
        rows = pl.ds(120, 96)
        return pltpu.make_async_copy(grad_ref.at[slabs, rows], grad_out.at[slabs, rows], down_sem.at[m])

    loads[0].wait()
    small = big_ref[:, 216:, :128].reshape(SLABS * 8, 128)
    b_out = spread_vector(small, 0, 0, SUB, WIDE)
    b_down = spread_vector(small, 1, 0, SUB, WIDE)

    parts = []
    for g in range(GROUPS):
        third = unpack_third(att_ref[g, TOK:].astype(F32))
        parts.append(jnp.concatenate([att_ref[g, :TOK].astype(F32), third], axis=1)[:, :192])

    def over_parts(values):
        total = jnp.sum(values[0], axis=1, keepdims=True)
        for value in values[1:]:
            total = total + jnp.sum(value, axis=1, keepdims=True)
        return total * (1.0 / WIDE)

    mean = over_parts(parts)
    parts = [part - mean for part in parts]
    att_scale = lax.rsqrt(over_parts([part * part for part in parts]) + epsilon)
    normed_att = [part * att_scale for part in parts]
    low_att = [part.astype(LOW) for part in normed_att]

    def out_rows(g):
        return big_ref[8 * g : 8 * g + 8, 0:SUB, :].reshape(192, WIDE)

    loads[1].wait()
    middle = x_ref[...] + b_out
    for g in range(GROUPS):
        middle = middle + dot_nn(low_att[g], out_rows(g))
    centre = middle - row_mean(middle)
    mid_scale = lax.rsqrt(row_mean(centre * centre) + epsilon)
    normed_mid = centre * mid_scale
    low_mid = normed_mid.astype(LOW)

    def in_cols(m):
        return big_ref[:, pl.ds(pl.multiple_of(SUB + SUB * m, 8), SUB), :].reshape(WIDE, WIDE)

    def down_rows(m):
        return big_ref[pl.ds(8 * m, 8), 120:216, :].reshape(WIDE, WIDE)

    def gelu_step(m, total):
        pre = dot_nn(low_mid, in_cols(m)) + spread_vector(small, 2, 8 * m, 96, WIDE)
        act = 0.5 * pre * (1.0 + lax.erf(pre * (2.0**-0.5)))
        pre_ref[m] = pre
        act_ref[m] = act
        return total + jnp.sum(act, axis=1, keepdims=True)

    loads[2].wait()
    zero_col = jnp.zeros((TOK, 1), F32)
    mean = lax.fori_loop(0, 4, gelu_step, zero_col) * (1.0 / (4 * WIDE))

    def spread_step(m, total):
        centre = act_ref[m] - mean
        act_ref[m] = centre
        return total + jnp.sum(centre * centre, axis=1, keepdims=True)

    inner_scale = lax.rsqrt(lax.fori_loop(0, 4, spread_step, zero_col) * (1.0 / (4 * WIDE)) + epsilon)
    g_out = cot_ref[...].astype(LOW)
    loads[3].wait()
    out_ref[...] = middle + b_down

    def down_step(m, sums):
        normed = act_ref[m] * inner_scale
        act_ref[m] = normed
        low = normed.astype(LOW)
        weights = down_rows(m)
        out_ref[...] += dot_nn(low, weights)
        grad = dot_tn(low, g_out)
        grad_ref[pl.ds(8 * m, 8), 120:216, :] = grad.astype(LOW).reshape(8, 96, WIDE)
        down_store(m).start()
        back = dot_nt(g_out, weights)
        gin_ref[m] = back
        return (
            sums[0] + jnp.sum(back, axis=1, keepdims=True),
            sums[1] + jnp.sum(back * normed, axis=1, keepdims=True),
        )

    sums = lax.fori_loop(0, 4, down_step, (zero_col, zero_col))
    first_mean = sums[0] * (1.0 / (4 * WIDE))
    second_mean = sums[1] * (1.0 / (4 * WIDE))

    def pre_step(m, state):
        back, small_rows = state
        g_act = inner_scale * (gin_ref[m] - first_mean - act_ref[m] * second_mean)
        pre = pre_ref[m]
        slope = 0.5 * (1.0 + lax.erf(pre * (2.0**-0.5))) + pre * jnp.exp(-0.5 * pre * pre) * (
            1.0 / math.sqrt(2.0 * math.pi)
        )
        g_pre = g_act * slope
        low = g_pre.astype(LOW)
        bias = jnp.sum(low.astype(F32), axis=0, keepdims=True)
        rows = jnp.where(iota((8, WIDE), 0) == 2, bias, 0.0)
        small_rows = small_rows + slab_rows(rows, 8 * m, 96, WIDE)
        grad = dot_tn(low_mid, low)
        at = pl.ds(pl.multiple_of(SUB + SUB * m, 8), SUB)
        grad_ref[:, at, :] = grad.astype(LOW).reshape(SLABS, SUB, WIDE)
        return (back + dot_nt(low, in_cols(m)), small_rows)

    back, small_rows = lax.fori_loop(
        0, 4, pre_step, (jnp.zeros((TOK, WIDE), F32), jnp.zeros((SLABS * 8, 128), F32))
    )
    stores[2].start()
    g_middle = cot_ref[...] + mid_scale * (back - row_mean(back) - normed_mid * row_mean(back * normed_mid))
    gmid_ref[...] = g_middle
    branch = g_middle.astype(LOW)
    at = iota((8, WIDE), 0)
    rows = jnp.where(at == 0, jnp.sum(branch.astype(F32), axis=0, keepdims=True), 0.0)
    rows = jnp.where(at == 1, jnp.sum(g_out.astype(F32), axis=0, keepdims=True), rows)
    small_rows = small_rows + slab_rows(rows, 0, SUB, WIDE)
    grad_ref[:, 216:, :] = jnp.zeros((SLABS, 8, WIDE), LOW)
    grad_ref[:, 216:, :128] = small_rows.astype(LOW).reshape(SLABS, 8, 128)
    stores[0].start()
    backs = []
    for g in range(GROUPS):
        grad = dot_tn(low_att[g], branch)
        grad_ref[8 * g : 8 * g + 8, 0:SUB, :] = grad.astype(LOW).reshape(8, SUB, WIDE)
        backs.append(dot_nt(branch, out_rows(g)))
    stores[1].start()
    first_mean = over_parts(backs)
    second_mean = over_parts([back * part for back, part in zip(backs, normed_att)])
    for g in range(GROUPS):
        g_att = att_scale * (backs[g] - first_mean - normed_att[g] * second_mean)
        wide_ref[:, :192] = g_att
        gatt_ref[g, :TOK] = wide_ref[:, :128].astype(LOW)
        gatt_ref[g, TOK:] = pack_third(wide_ref[:, 128:]).astype(LOW)
    for copy in stores:
        copy.wait()
    for m in range(4):
        down_store(m).wait()


class Scatter:
    def __init__(self, place, grad_ref, acc_ref, spaces, own_sems, send_sems, recv_sems, first):
        self.p, self.grad, self.acc = place, grad_ref, acc_ref
        self.r1, self.s1x, self.s1y, self.s3x, self.s3y, self.zu, self.zd = spaces
        self.own, self.send, self.recv = own_sems, send_sems, recv_sems
        self.diagonal = 3 - place.dp
        self.begin, self.half = first, PIECE // 2
        self.rows, self.small = pl.ds(first, PIECE), pl.ds(first // 2, PIECE // 2)

    def copy(self, src, dst, kind, item, peer):
        return remote(src, dst, self.send.at[kind, item], self.recv.at[kind, item], peer)

    def own_copy(self, item):
        return pltpu.make_async_copy(
            self.grad.at[:, self.p.c, item, self.rows], self.acc.at[:, item, self.rows], self.own.at[item]
        )

    def core_copy(self, item):
        src = self.grad.at[:, self.p.cn, item, self.rows]
        return self.copy(src, self.r1.at[:, item, self.rows], 0, item, {"ctx": self.p.cn})

    def first_copies(self, item):
        one = self.acc.at[self.diagonal, item, pl.ds(self.begin, self.half)]
        two = self.acc.at[self.diagonal, item, pl.ds(self.begin + self.half, self.half)]
        return (
            self.copy(one, self.s1y.at[item, self.small], 1, item, {"dp": self.p.yn}),
            self.copy(two, self.s1x.at[item, self.small], 2, item, {"dp": self.p.xn}),
        )

    def second_copies(self, item):
        return tuple(
            self.copy(self.acc.at[to, item, self.rows], space.at[item, self.rows], kind, item, {"dp": to})
            for to, space, kind in ((self.p.xn, self.s3x, 3), (self.p.yn, self.s3y, 4))
        )

    def z_copy(self, item, up):
        to = lax.rem(self.p.h + (1 if up else GROUPS - 1), GROUPS)
        space = self.zu if up else self.zd
        src = self.acc.at[self.p.dp, item, self.rows]
        return self.copy(src, space.at[item, self.rows], 5 if up else 6, item, {"head": to})

    def start(self, item):
        self.core_copy(item).start()
        self.own_copy(item).start()

    def add(self, at_dp, item, first, source, rows, others):
        @pl.loop(0, rows // 8)
        def _(step):
            to = pl.ds(pl.multiple_of(first + step * 8, 8), 8)
            of = pl.ds(pl.multiple_of(source + step * 8, 8), 8)
            total = self.acc[at_dp, item, to, :].astype(F32)
            for other in others:
                total = total + other[item, of, :].astype(F32)
            self.acc[at_dp, item, to, :] = total.astype(LOW)

    def cores(self, item):
        self.own_copy(item).wait()
        self.core_copy(item).wait_recv()

        @pl.loop(0, PIECE // 8)
        def _(step):
            at = pl.ds(pl.multiple_of(self.begin + step * 8, 8), 8)
            total = self.acc[:, item, at, :].astype(F32) + self.r1[:, item, at, :].astype(F32)
            self.acc[:, item, at, :] = total.astype(LOW)

        for copy in self.first_copies(item):
            copy.start()

    def first(self, item):
        for copy in self.first_copies(item):
            copy.wait_recv()
        begin, half = self.begin, self.half
        self.add(self.p.xn, item, begin, begin // 2, half, (self.s1y,))
        self.add(self.p.yn, item, begin + half, begin // 2, half, (self.s1x,))
        for copy in self.second_copies(item):
            copy.start()

    def second(self, item):
        for copy in self.second_copies(item):
            copy.wait_recv()
        self.add(self.p.dp, item, self.begin, self.begin, PIECE, (self.s3x, self.s3y))

    def along_z(self, item, hop):
        for up, here in ((True, hop < item), (False, GROUPS - 1 - hop > item)):
            if not here:
                continue
            at = hop if up else GROUPS - 1 - hop

            @pl.when(self.p.h == at)
            def _():
                copy = self.z_copy(item, up)
                if hop:
                    copy.wait_recv()
                    self.add(self.p.dp, item, self.begin, self.begin, PIECE, (self.zu if up else self.zd,))
                copy.start()

    def finish(self, out_ref):
        h = self.p.h
        out_ref[self.rows, :] = self.acc[self.p.dp, h, self.rows, :].astype(F32)
        for up, there in ((True, h > 0), (False, h < GROUPS - 1)):

            @pl.when(there)
            def _():
                self.z_copy(h, up).wait_recv()
                out_ref[self.rows, :] += (self.zu if up else self.zd)[h, self.rows, :].astype(F32)

        for item in range(GROUPS):
            self.core_copy(item).wait_send()
            for copy in self.first_copies(item) + self.second_copies(item):
                copy.wait_send()
            for up, there in ((True, h < item), (False, h > item)):
                pl.when(there)(self.z_copy(item, up).wait_send)


def backward_kernel(
    offs_ref, gatt_ref, o_ref, lse_ref, xall_in, qkv_in, wg_in, grad_ref,
    gx_ref, rs_ref, rq_ref,
    xall_ref, qkv_ref, wg_ref, load_sem, now_ref, gat_ref, dk_ref, dv_ref, g3_ref, dq_ref, wcat_ref, dw_ref, bias_ref, slab_ref,
    part_ref, precv_ref, psum_ref, pu_ref, pd_ref,
    acc_ref, r1_ref, s1x_ref, s1y_ref, s3x_ref, s3y_ref, zu_ref, zd_ref, q0_ref, q1_ref, q2_ref, q3_ref, q4_ref,
    gs, gr, ps, pr, pzs, pzu, pzd, os, bs, br, qs, qr,
):
    place = Place()
    dp, c, h = place.dp, place.c, place.h
    own = c * GROUPS + h
    loads = [
        pltpu.make_async_copy(src, dst, load_sem.at[at])
        for at, (src, dst) in enumerate(((wg_in, wg_ref), (qkv_in, qkv_ref), (xall_in, xall_ref)))
    ]
    for copy in loads:
        copy.start()
    enter(place)
    core = place.core_of(own)
    slot = c * 2 + jnp.where(lax.rem(own, 4) >= 2, 1, 0)
    sent = []
    for part in range(GROUPS):
        away = jnp.logical_or(core != c, h != part)
        copy = remote(
            gatt_ref.at[part], gat_ref.at[slot], gs.at[part], gr.at[slot], {"ctx": core, "head": part}
        )
        sent.append((away, copy))
        pl.when(away)(copy.start)

        @pl.when(jnp.logical_not(away))
        def _():
            gat_ref[slot] = gatt_ref[part]

    spaces = (r1_ref, s1x_ref, s1y_ref, s3x_ref, s3y_ref, zu_ref, zd_ref)
    bigs = [
        Scatter(place, grad_ref, acc_ref, spaces, os.at[at], bs.at[at], br.at[at], first)
        for at, first in enumerate(range(0, BIG_ROWS, PIECE))
    ]

    def sums_step(name, *item):
        for big in bigs:
            getattr(big, name)(*item)

    order = (3, 0, 2, 1)
    for item in order:
        sums_step("start", item)
    for copy in loads:
        copy.wait()
    wcat_ref[...] = wg_ref[:, :SUB, :].reshape(WIDE, WIDE)

    @pl.loop(0, 8)
    def _(block):
        dk_ref[block] = jnp.zeros((TOK, LANES), F32)
        dv_ref[block] = jnp.zeros((TOK, LANES), F32)
        g3_ref[block] = jnp.zeros((TOK, WIDE), LOW)

    for item in order:
        sums_step("cores", item)
    low, high = head_masks()

    def attend_back(i):
        block = place.q_block(i)
        count_tables(offs_ref, now_ref, h, block, True, 0, 2 * i + 2)
        local = block == own
        copy = remote(gatt_ref.at[0], gat_ref.at[i], gs.at[0], gr.at[i], {"ctx": place.cn})
        pl.when(jnp.logical_not(local))(copy.wait_recv)
        third = jnp.where(low, unpack_third(gat_ref[i, TOK:].astype(F32)), 0.0)
        both = jnp.concatenate([gat_ref[i, :TOK], third.astype(LOW)], axis=1)
        outs = split_heads(both)
        queries = split_heads(qkv_ref[block, :, :LANES])
        product = both.astype(F32) * o_ref[i].astype(F32)
        pieces = (
            jnp.where(low, product[:, :128], 0.0),
            jnp.where(high, product[:, :128], 0.0),
            product[:, 128:],
        )
        deltas = [
            jnp.broadcast_to(jnp.sum(piece, axis=1, keepdims=True), (TOK, 128)).T[:1] for piece in pieces
        ]
        lses = [lse_ref[i, j, :1] for j in range(3)]
        dq_ref[...] = jnp.zeros_like(dq_ref)

        @pl.loop(0, 2 * i + 2)
        def _(key):
            @pl.when(key <= block)
            def _():
                keys = qkv_ref[key, :, LANES : 2 * LANES]
                values = qkv_ref[key, :, 2 * LANES :]
                tile_k = (keys[:, :128], keys[:, :128], keys[:, 128:])
                tile_v = (values[:, :128], values[:, :128], values[:, 128:])
                dks = []
                dvs = []
                for j in range(3):
                    scores = dot_nt(tile_k[j], queries[j])
                    probs = jnp.exp(scores - lses[j]) * now_ref[j, key]
                    dvs.append(dot_nn(probs.astype(LOW), outs[j]))
                    g_probs = dot_nt(tile_v[j], outs[j])
                    g_scores = (probs * (g_probs - deltas[j])).astype(LOW)
                    dks.append(dot_nn(g_scores, queries[j]))
                    dq_ref[j] += dot_tn(g_scores, tile_k[j])
                dk_ref[key, :, :128] += dks[0] + dks[1]
                dk_ref[key, :, 128:] += dks[2]
                dv_ref[key, :, :128] += dvs[0] + dvs[1]
                dv_ref[key, :, 128:] += dvs[2]

        g3_ref[block, :, :128] = (jnp.where(low, dq_ref[0], dq_ref[1]) * 0.125).astype(LOW)
        g3_ref[block, :, 128:LANES] = (dq_ref[2] * 0.125).astype(LOW)

    def pair_copy(i):
        return remote(
            part_ref.at[pl.ds(2 * i, 2)], precv_ref.at[pl.ds(2 * (i % 2), 2)], ps.at[i], pr.at[i], {"ctx": place.cn}
        )

    def give_pair(i):
        @pl.loop(2 * i, 2 * i + 2)
        def _(block):
            g3_ref[block, :, LANES : 2 * LANES] = dk_ref[block].astype(LOW)
            g3_ref[block, :, 2 * LANES :] = dv_ref[block].astype(LOW)
            part_ref[block] = dot_nt(g3_ref[block], wcat_ref[...]).astype(LOW)

        pl.when(c != i // 2)(pair_copy(i).start)

    def take_pair(i):
        @pl.when(c == i // 2)
        def _():
            pair_copy(i).wait_recv()

            @pl.loop(0, 2)
            def _(k):
                at = 2 * (i % 2) + k
                total = part_ref[2 * i + k].astype(F32) + precv_ref[at].astype(F32)
                psum_ref[at] = total.astype(LOW)

    def pair_z(item, up):
        to = lax.rem(h + (1 if up else GROUPS - 1), GROUPS)
        space, sems = (pu_ref, pzu) if up else (pd_ref, pzd)
        return remote(psum_ref.at[item], space.at[item], pzs.at[item], sems.at[item], {"head": to})

    def pair_along(i, hop):
        for item in (2 * (i % 2), 2 * (i % 2) + 1):
            for up, here in ((True, hop < item), (False, GROUPS - 1 - hop > item)):
                if not here:
                    continue
                at = hop if up else GROUPS - 1 - hop

                @pl.when(jnp.logical_and(c == i // 2, h == at))
                def _():
                    copy = pair_z(item, up)
                    if hop:
                        copy.wait_recv()
                        total = psum_ref[item].astype(F32) + (pu_ref if up else pd_ref)[item].astype(F32)
                        psum_ref[item] = total.astype(LOW)
                    copy.start()

    sums_step("first", 3)
    attend_back(3)
    give_pair(3)
    sums_step("first", 0)
    sums_step("first", 2)
    take_pair(3)
    pair_along(3, 0)
    attend_back(2)
    give_pair(2)
    sums_step("first", 1)
    sums_step("second", 3)
    sums_step("along_z", 3, 0)
    pair_along(3, 1)
    take_pair(2)
    pair_along(2, 0)
    attend_back(1)
    give_pair(1)
    sums_step("second", 0)
    sums_step("along_z", 0, 0)
    pair_along(3, 2)
    pair_along(2, 1)
    sums_step("along_z", 3, 1)
    take_pair(1)
    pair_along(1, 0)
    attend_back(0)
    give_pair(0)
    dw_ref[...] = jnp.zeros_like(dw_ref)
    bias_ref[...] = jnp.zeros_like(bias_ref)

    @pl.loop(0, 8)
    def _(block):
        grads = g3_ref[block]
        bias_ref[...] += jnp.sum(grads.astype(F32).reshape(TOK // 8, 8, WIDE), axis=0)
        dw_ref[...] += dot_tn(xall_ref[block], grads)

    slab_ref[:, :SUB, :] = dw_ref[...].astype(LOW).reshape(SLABS, SUB, WIDE)
    sums = jnp.sum(bias_ref[...], axis=0, keepdims=True)
    used = iota((8, LANES), 1) < 192
    at = iota((8, LANES), 0)
    rows = jnp.where(jnp.logical_and(used, at == 0), sums[:, :LANES], 0.0)
    rows = jnp.where(jnp.logical_and(used, at == 1), sums[:, 2 * LANES :], rows)
    slab_ref[:, SUB:, :] = jnp.zeros((SLABS, 8, WIDE), LOW)
    slab_ref[:, SUB:, :128] = slab_rows(rows, 8 * h, SUB, LANES).astype(LOW).reshape(SLABS, 8, 128)
    q_steps = small_scatter(
        place, slab_ref, q0_ref, os.at[2], (q1_ref, q2_ref, None, q3_ref, None, q4_ref), rq_ref,
        qs, qr, ((0, QKV_ROWS),), False,
    )
    next(q_steps)
    take_pair(0)
    pair_along(0, 0)
    sums_step("second", 2)
    sums_step("along_z", 2, 0)
    pair_along(1, 1)
    pair_along(2, 2)
    next(q_steps)
    sums_step("along_z", 0, 1)
    sums_step("along_z", 3, 2)
    pair_along(0, 1)
    pair_along(1, 2)
    next(q_steps)
    pair_along(0, 2)
    next(q_steps)
    sums_step("second", 1)
    sums_step("along_z", 1, 0)
    sums_step("along_z", 0, 2)
    sums_step("along_z", 2, 1)
    sums_step("along_z", 1, 1)
    gx_ref[...] = psum_ref[h].astype(F32)
    for up, there in ((True, h > 0), (False, h < GROUPS - 1)):

        @pl.when(there)
        def _():
            pair_z(h, up).wait_recv()
            gx_ref[...] += (pu_ref if up else pd_ref)[h].astype(F32)

    sums_step("along_z", 2, 2)
    sums_step("along_z", 1, 2)
    for _ in q_steps:
        pass
    for part in range(GROUPS):
        pl.when(sent[part][0])(sent[part][1].wait_send)
        pl.when(c != part // 2)(pair_copy(part).wait_send)
        for up, there in ((True, h < part), (False, h > part)):
            pl.when(there)(pair_z(part, up).wait_send)
    sums_step("finish", rs_ref)


def small_scatter(place, grad_ref, acc_ref, own_sem, spaces, out_ref, bs, br, halves, summed):
    r1, r2a, r2b, r3a, r3b, r4 = spaces
    dp, c, h = place.dp, place.c, place.h
    x, y = place.x, place.y
    count = [0]

    def send(src, dst, peer):
        at = count[0]
        count[0] += 1
        copy = remote(src, dst, bs.at[at], br.at[at], peer)
        copy.start()
        return copy

    def slabs(at_dp, at_c):
        return pl.ds(at_dp * 8 + at_c * GROUPS, GROUPS)

    def add(at_dp, first, last, got):
        @pl.loop(0, (last - first) // 8)
        def _(step):
            to = pl.ds(pl.multiple_of(first + step * 8, 8), 8)
            of = pl.ds(pl.multiple_of(step * 8, 8), 8)
            total = acc_ref[at_dp, :, to, :].astype(F32) + got[:, of, :].astype(F32)
            acc_ref[at_dp, :, to, :] = total.astype(LOW)

    own_copies = [
        pltpu.make_async_copy(grad_ref.at[slabs(d, c)], acc_ref.at[d], own_sem.at[d]) for d in range(4)
    ]
    for copy in own_copies:
        copy.start()
    stage = [send(grad_ref.at[slabs(d, place.cn)], r1.at[d], {"ctx": place.cn}) for d in range(4)]
    yield
    for copy in own_copies:
        copy.wait()
    for copy in stage:
        copy.wait()
    for d in range(4):
        add(d, halves[0][0], halves[-1][1], r1.at[d])
    ones = [halves[i] for i in range(0, len(halves), 2)]
    twos = [halves[i] for i in range(1, len(halves), 2)]

    def span(bounds):
        return pl.ds(bounds[0], bounds[1] - bounds[0])

    def x_side(q):
        return 2 * q + 1 - x

    def y_side(q):
        return 2 * (1 - y) + q

    stage = []
    at = 0
    for bounds in ones:
        size = bounds[1] - bounds[0]
        for q in range(2):
            stage.append(send(acc_ref.at[x_side(q), :, span(bounds)], r2a.at[q, :, pl.ds(at, size)], {"dp": place.xn}))
        at += size
    at = 0
    for bounds in twos:
        size = bounds[1] - bounds[0]
        for q in range(2):
            stage.append(send(acc_ref.at[y_side(q), :, span(bounds)], r2b.at[q, :, pl.ds(at, size)], {"dp": place.yn}))
        at += size
    yield
    for copy in stage:
        copy.wait()
    at = 0
    for bounds in ones:
        size = bounds[1] - bounds[0]
        for q in range(2):
            add(2 * q + x, *bounds, r2a.at[q, :, pl.ds(at, size)])
        at += size
    at = 0
    for bounds in twos:
        size = bounds[1] - bounds[0]
        for q in range(2):
            add(2 * y + q, *bounds, r2b.at[q, :, pl.ds(at, size)])
        at += size
    stage = []
    at = 0
    for bounds in ones:
        size = bounds[1] - bounds[0]
        stage.append(send(acc_ref.at[place.yn, :, span(bounds)], r3a.at[:, pl.ds(at, size)], {"dp": place.yn}))
        at += size
    at = 0
    for bounds in twos:
        size = bounds[1] - bounds[0]
        stage.append(send(acc_ref.at[place.xn, :, span(bounds)], r3b.at[:, pl.ds(at, size)], {"dp": place.xn}))
        at += size
    yield
    for copy in stage:
        copy.wait()
    at = 0
    for bounds in ones:
        size = bounds[1] - bounds[0]
        add(dp, *bounds, r3a.at[:, pl.ds(at, size)])
        at += size
    at = 0
    for bounds in twos:
        size = bounds[1] - bounds[0]
        add(dp, *bounds, r3b.at[:, pl.ds(at, size)])
        at += size
    stage = [send(acc_ref.at[dp, place.z(k)], r4.at[k - 1], {"head": place.z(k)}) for k in (1, 2, 3)]
    yield
    for copy in stage:
        copy.wait()
    if summed:
        total = acc_ref[dp, h].astype(F32)
        for k in range(3):
            total = total + r4[k].astype(F32)
        out_ref[...] = total
    else:
        out_ref[h] = acc_ref[dp, h].astype(F32)
        for k in (1, 2, 3):
            out_ref[place.z_from(k)] = r4[k - 1].astype(F32)


RS_SEMS = 4 + 8 + 4 + 3


def vmem(count):
    return [pl.BlockSpec(memory_space=pltpu.VMEM)] * count


def fast_device(
    inputs, cotangent, head_offsets, w_qkv, b_query, b_value, w_out, b_out, w_in, b_in, w_down, b_down,
    gain_pre, gain_attn, gain_ffn_pre, gain_ffn_mid,
):
    rows = inputs.reshape(TOK, WIDE)
    cot = cotangent.reshape(TOK, WIDE)
    dma = pltpu.SemaphoreType.DMA
    sds = jax.ShapeDtypeStruct

    weights = (w_qkv, w_out, w_in, w_down)
    gains = tuple(v[None] for v in (gain_pre, gain_attn, gain_ffn_pre, gain_ffn_mid))
    biases = tuple(v[None] for v in (b_query, b_value, b_out, b_in, b_down))
    spec = pl.BlockSpec(memory_space=pltpu.VMEM)
    xall, qkv, wg, big, outs, lse, att = pl.pallas_call(
        forward_kernel,
        name="attention_forward",
        out_shape=(
            sds((8, TOK, WIDE), LOW),
            sds((8, TOK, WIDE), LOW),
            sds((4, CORES, GROUPS, QKV_ROWS, WIDE), LOW),
            sds((4, CORES, GROUPS, BIG_ROWS, WIDE), LOW),
            sds((PARTS, TOK, LANES), LOW),
            sds((PARTS, 3, 8, TOK), F32),
            sds((GROUPS, TOK + TOK // 2, 128), LOW),
        ),
        in_specs=[pl.BlockSpec(memory_space=pltpu.SMEM)] + vmem(5) + [(spec,) * 4, (spec,) * 5],
        out_specs=(pl.BlockSpec(memory_space=pl.ANY),) * 4 + tuple(vmem(3)),
        scratch_shapes=[
            pltpu.VMEM((PARTS, TOK + TOK // 2, 128), LOW),
            pltpu.VMEM((8, TOK, WIDE), LOW),
            pltpu.VMEM((8, TOK, WIDE), LOW),
            pltpu.VMEM((4, CORES, GROUPS, QKV_ROWS, WIDE), LOW),
            dma((3,)),
            pltpu.VMEM((GROUPS, QKV_ROWS, WIDE), LOW),
            pltpu.VMEM((BIG_ROWS, WIDE), LOW),
            pltpu.VMEM((8, WIDE), F32),
            pltpu.VMEM((3, 20, TOK, TOK), F32),
            pltpu.VMEM((3, 8, TOK, TOK), F32),
            pltpu.VMEM((3, TOK, TOK), F32),
            pltpu.VMEM((3, TOK, 128), F32),
            pltpu.VMEM((WIDE, WIDE), LOW),
            dma(()),
            *[dma((4,)) for _ in range(5)], dma((6,)), dma((6,)), dma((4,)), dma((4,)),
            *[dma((4,)) for _ in range(2 * GATHER_SEMS)],
        ],
        compiler_params=pltpu.CompilerParams(
            collective_id=0, has_side_effects=True, vmem_limit_bytes=60 * 1024 * 1024
        ),
    )(head_offsets, rows, *weights, gains, biases)
    out, g_middle, g_att, grads = pl.pallas_call(
        middle_kernel,
        name="ffn_both_ways",
        out_shape=(
            sds((TOK, WIDE), F32),
            sds((TOK, WIDE), F32),
            sds((GROUPS, TOK + TOK // 2, 128), LOW),
            sds((SLABS, BIG_ROWS, WIDE), LOW),
        ),
        in_specs=vmem(3) + [pl.BlockSpec(memory_space=pl.ANY)],
        out_specs=tuple(vmem(3)) + (pl.BlockSpec(memory_space=pl.ANY),),
        scratch_shapes=[
            pltpu.VMEM((SLABS, BIG_ROWS, WIDE), LOW),
            pltpu.VMEM((SLABS, BIG_ROWS, WIDE), LOW),
            pltpu.VMEM((4, TOK, WIDE), F32),
            pltpu.VMEM((4, TOK, WIDE), F32),
            pltpu.VMEM((4, TOK, WIDE), F32),
            pltpu.VMEM((TOK, LANES), F32),
            dma((4,)), dma((3,)), dma((4,)),
        ],
        compiler_params=pltpu.CompilerParams(vmem_limit_bytes=60 * 1024 * 1024),
    )(rows, cot, att, big.reshape(SLABS, BIG_ROWS, WIDE))
    back, rs, rq = pl.pallas_call(
        backward_kernel,
        name="attention_backward",
        out_shape=(
            sds((TOK, WIDE), F32),
            sds((BIG_ROWS, WIDE), F32),
            sds((GROUPS, QKV_ROWS, WIDE), F32),
        ),
        in_specs=[pl.BlockSpec(memory_space=pltpu.SMEM)] + vmem(3) + [pl.BlockSpec(memory_space=pl.ANY)] * 4,
        out_specs=tuple(vmem(3)),
        scratch_shapes=[
            pltpu.VMEM((8, TOK, WIDE), LOW),
            pltpu.VMEM((8, TOK, WIDE), LOW),
            pltpu.VMEM((SLABS, QKV_ROWS, WIDE), LOW),
            dma((3,)),
            pltpu.VMEM((3, 8, TOK, TOK), F32),
            pltpu.VMEM((PARTS, TOK + TOK // 2, 128), LOW),
            pltpu.VMEM((8, TOK, LANES), F32),
            pltpu.VMEM((8, TOK, LANES), F32),
            pltpu.VMEM((8, TOK, WIDE), LOW),
            pltpu.VMEM((3, TOK, 128), F32),
            pltpu.VMEM((WIDE, WIDE), LOW),
            pltpu.VMEM((WIDE, WIDE), F32),
            pltpu.VMEM((8, WIDE), F32),
            pltpu.VMEM((SLABS, QKV_ROWS, WIDE), LOW),
            pltpu.VMEM((8, TOK, WIDE), LOW),
            *[pltpu.VMEM((GROUPS, TOK, WIDE), LOW) for _ in range(4)],
            pltpu.VMEM((4, GROUPS, BIG_ROWS, WIDE), LOW),
            pltpu.VMEM((4, GROUPS, BIG_ROWS, WIDE), LOW),
            *[pltpu.VMEM((GROUPS, BIG_ROWS // 2, WIDE), LOW) for _ in range(2)],
            *[pltpu.VMEM((GROUPS, BIG_ROWS, WIDE), LOW) for _ in range(4)],
            pltpu.VMEM((4, GROUPS, QKV_ROWS, WIDE), LOW),
            pltpu.VMEM((4, GROUPS, QKV_ROWS, WIDE), LOW),
            pltpu.VMEM((2, GROUPS, QKV_ROWS, WIDE), LOW),
            pltpu.VMEM((GROUPS, QKV_ROWS, WIDE), LOW),
            pltpu.VMEM((3, QKV_ROWS, WIDE), LOW),
            *[dma((4,)) for _ in range(7)], dma((3, 4)), dma((2, 7, 4)), dma((2, 7, 4)), dma((RS_SEMS,)), dma((RS_SEMS,)),
        ],
        compiler_params=pltpu.CompilerParams(
            collective_id=1, has_side_effects=True, vmem_limit_bytes=63 * 1024 * 1024
        ),
    )(
        head_offsets, g_att, outs, lse, xall, qkv, wg.reshape(SLABS, QKV_ROWS, WIDE),
        grads.reshape(4, CORES, GROUPS, BIG_ROWS, WIDE),
    )

    sizes = (SUB, SUB, SUB, 4 * SUB, SUB, SUB, SUB, SUB, 4 * SUB)
    gx, grads, vectors = pl.pallas_call(
        finish_kernel,
        name="parameter_outputs",
        out_shape=(
            sds((TOK, WIDE), F32), tuple(sds(v.shape, F32) for v in weights), tuple(sds((1, size), F32) for size in sizes)
        ),
        in_specs=vmem(9) + [(spec,) * 4],
        out_specs=(spec, (spec,) * 4, (spec,) * 9),
    )(rows, g_middle, back, rs, rq, *weights, gains)
    v_query, v_value, v_out, v_in, v_down, v_pre, v_attn, v_ffn, v_mid = [v[0] for v in vectors]
    return (
        out.reshape(inputs.shape),
        gx.reshape(inputs.shape),
        grads[0],
        v_query,
        v_value,
        grads[1],
        v_out,
        grads[2],
        v_in,
        grads[3],
        v_down,
        v_pre,
        v_attn,
        v_ffn,
        v_mid,
    )


def per_device(*args):
    inputs, w_in = args[0], args[8]
    sizes = tuple(lax.axis_size(axis) for axis in ("dp", "ctx", "head"))
    same = sizes == (4, CORES, GROUPS) and inputs.shape == (1, TOK, WIDE) and w_in.shape == (SUB, 4 * WIDE)
    return fast_device(*args) if same else general_device(*args)


def solution(mesh):
    placed = (
        P("dp", ("ctx", "head"), None),
        P("dp", ("ctx", "head"), None),
        P(),
        P(("dp", "ctx", "head"), None),
        P(("dp", "ctx", "head")),
        P(("dp", "ctx", "head")),
        P(("dp", "ctx", "head"), None),
        P(("dp", "ctx", "head")),
        P(("dp", "ctx", "head"), None),
        P(("dp", "ctx", "head")),
        P(("dp", "ctx", "head"), None),
        P(("dp", "ctx", "head")),
        P(("dp", "ctx", "head")),
        P(("dp", "ctx", "head")),
        P(("dp", "ctx", "head")),
        P(("dp", "ctx", "head")),
    )
    return jax.shard_map(
        per_device,
        mesh=mesh,
        in_specs=placed,
        out_specs=(
            P("dp", ("ctx", "head"), None),
            P("dp", ("ctx", "head"), None),
            P(("dp", "ctx", "head"), None),
            P(("dp", "ctx", "head")),
            P(("dp", "ctx", "head")),
            P(("dp", "ctx", "head"), None),
            P(("dp", "ctx", "head")),
            P(("dp", "ctx", "head"), None),
            P(("dp", "ctx", "head")),
            P(("dp", "ctx", "head"), None),
            P(("dp", "ctx", "head")),
            P(("dp", "ctx", "head")),
            P(("dp", "ctx", "head")),
            P(("dp", "ctx", "head")),
            P(("dp", "ctx", "head")),
        ),
        check_vma=False,
    )
```
